32 devices in a mesh: row: 8 (over z, x), col: 4 (over y, core).
Axes of the slice: x: 2, y: 2, z: 4, core: 2. Of those that a mesh axis runs over, the one named last changes fastest.
Arguments:
- inputs: bfloat16 [8192, 768], P(('row', 'col')), may hold values from -6 to 6
- doc_lengths: int32 [8, 6], P('row'), may hold values from 1 to 512, 1024 in all within a row
- weight_query: bfloat16 [768, 768], P('row', 'col'), may hold values from -0.21875 to 0.21875
- weight_key: bfloat16 [768, 768], P('row', 'col'), may hold values from -0.21875 to 0.21875
- weight_value: bfloat16 [768, 768], P('row', 'col'), may hold values from -0.21875 to 0.21875
- bias_query: float32 [768], P('col'), may hold values from -3 to 3
- bias_value: float32 [768], P('col'), may hold values from -3 to 3
- weight_out: bfloat16 [768, 768], P('col', 'row'), may hold values from -1.25 to 1.25
- bias_out: float32 [768], replicated, may hold values from -3 to 3
- norm_gain: float32 [768], replicated, may hold values from 0.5 to 1.5
- norm_shift: float32 [768], replicated, may hold values from -2 to 2
- weight_up: bfloat16 [768, 3072], P('row', 'col'), may hold values from -0.21875 to 0.21875
- bias_up: float32 [3072], P('col'), may hold values from -3 to 3
- weight_down: bfloat16 [3072, 768], P('col', 'row'), may hold values from -0.109375 to 0.109375
- bias_down: float32 [768], replicated, may hold values from -2 to 2
- final_gain: float32 [768], replicated, may hold values from 0.5 to 1.5
- final_shift: float32 [768], replicated, may hold values from -2 to 2
- cotangent: bfloat16 [8192, 768], P(('row', 'col')), may hold values from -6 to 6
Outputs:
- output: bfloat16 [8192, 768], P(('row', 'col'))
- grad_input: float32 [8192, 768], P(('row', 'col'))
- grad_query: float32 [768, 768], P('row', 'col')
- grad_key: float32 [768, 768], P('row', 'col')
- grad_value: float32 [768, 768], P('row', 'col')
- grad_query_bias: float32 [768], P('col')
- grad_value_bias: float32 [768], P('col')
- grad_out: float32 [768, 768], P('col', 'row')
- grad_out_bias: float32 [768], replicated
- grad_norm_gain: float32 [768], replicated
- grad_norm_shift: float32 [768], replicated
- grad_up: float32 [768, 3072], P('row', 'col')
- grad_up_bias: float32 [3072], P('col')
- grad_down: float32 [3072, 768], P('col', 'row')
- grad_down_bias: float32 [768], replicated
- grad_final_gain: float32 [768], replicated
- grad_final_shift: float32 [768], replicated
The draws below stay inside these ranges and needn't reach their ends.
Inputs may be any that keep to these rules, and one draw needn't show every extreme that they name: `doc_lengths`: each row holds the lengths of the 6 documents packed into one sequence, in order; every row sums to 1024 and its largest entry is 512.
All inputs are finite; a program needn't handle non-finite values.
Results may differ from the reference program's by a relative error of at most 0.013.
Values may be sent and summed in bfloat16 or wider, within the bound.
No kernel may reach another device: no remote copies, remote signals or barrier semaphores. Data moves between devices by JAX's collectives and lax.ppermute only.
A program may use at most 128 MiB of HBM per device.

```python
import math
import jax
import jax.numpy as jnp
import numpy as np
from jax import lax

D = 768
HEADS = 12
HEAD_DIM = 64
FF = 3072
TOK_DEV = 1024
DOCS = 6
DOC_MOST = 512
SEQS = 8
TOKENS = 8192


def spiked(drawn, key, source, target, shards_of, factor):
    def block_of(position):
        return (jnp.arange(drawn.shape[position]) // (drawn.shape[position] // shards_of)).reshape((-1,) + (1,) * (drawn.ndim - 1 - position))

    first = jax.random.permutation(key, shards_of)[block_of(target)]
    other_side = (block_of(target) + shards_of // 2) % shards_of
    return jnp.where((block_of(source) == first) | (block_of(source) == other_side), factor * drawn, drawn)


def shard_levels(key, extent, split, least, top_value):
    def one(position, blocks):
        draws = jax.random.uniform(jax.random.fold_in(jax.random.fold_in(key, 6), position), (blocks,), jnp.float32, least / len(split), top_value / len(split))
        return jnp.repeat(jnp.exp(draws), extent[position] // blocks).reshape((-1,) + (1,) * (len(extent) - position - 1))

    loudness = one(*split[0])
    for cut in split[1:]:
        loudness = loudness * one(*cut)
    return loudness


def split_up(number_of, total, limit, slope):
    portions = [(1 << 20) // math.isqrt(rank ** slope) + 1 for rank in range(2, number_of + 1)]
    rest, counts = total - limit - (number_of - 1), [1] * (number_of - 1)
    while rest > 0:
        free = [i for i in range(number_of - 1) if counts[i] < limit]
        mass, remaining = sum([portions[i] for i in free]), rest
        for i in free:
            more = min(limit - counts[i], max(1, remaining * portions[i] // mass), rest)
            counts[i] = counts[i] + more
            rest = rest - more
    return np.array([limit] + counts)


def ragged(key, number_of, total, most, lean):
    if number_of == 2:
        one = jax.random.randint(key, (), max(1, total - most), min(most, total - 1) + 1)
        return jnp.stack([one, total - one])
    sizes = jnp.asarray(split_up(number_of, total, most, lean), jnp.int32)
    pairs = (number_of - 1) // 2
    donor, taker = sizes[1:1 + 2 * pairs:2], sizes[2:2 + 2 * pairs:2]
    margin = jnp.minimum(donor - 1, most - taker)
    shifted = jax.random.randint(jax.random.fold_in(key, 1), (pairs,), 0, 1 << 20) % (margin + 1)
    sizes = sizes.at[1:1 + 2 * pairs:2].set(donor - shifted).at[2:2 + 2 * pairs:2].set(taker + shifted)
    return sizes[jax.random.permutation(jax.random.fold_in(key, 2), number_of)]


def gaussian(rng, dims, spread, limit, pieces=(), kind=jnp.bfloat16):
    level = shard_levels(rng, dims, pieces, -0.22, 0.18) if pieces else 1.0
    values = jax.random.normal(rng, dims, jnp.float32) * spread * level
    return jnp.minimum(jnp.maximum(values, -limit), limit).astype(kind)


def gaussian_with(rng, shape, width, limit, shards, heavy, held_as=jnp.bfloat16):
    values = width * jax.random.normal(rng, shape, jnp.float32)
    if shards:
        values = values * shard_levels(rng, shape, shards, -0.22, 0.18)
    return jnp.clip(spiked(values, jax.random.fold_in(rng, 3), *heavy), -limit, limit).astype(held_as)


def setup_inputs(seed: int = 0) -> dict:
    seeds = jax.random.split(jax.random.key(seed), 19)
    inputs = gaussian(seeds[0], (TOKENS, D), 1.0, 6.0, ((0, 32),))
    doc_lengths = jax.vmap(lambda own: ragged(own, DOCS, TOK_DEV, DOC_MOST, 2))(jax.random.split(seeds[1], SEQS)).reshape((SEQS, DOCS)).astype(jnp.int32)
    weight_query = gaussian(seeds[2], (D, D), D ** -0.5, 0.21875, ((0, 8), (1, 4)))
    weight_key = gaussian(seeds[3], (D, D), D ** -0.5, 0.21875, ((0, 8), (1, 4)))
    weight_value = gaussian(seeds[4], (D, D), D ** -0.5, 0.21875, ((0, 8), (1, 4)))
    bias_query = gaussian(seeds[5], (D,), 0.5, 3.0, ((0, 4),), jnp.float32)
    bias_value = gaussian(seeds[6], (D,), 0.5, 3.0, ((0, 4),), jnp.float32)
    weight_out = gaussian(seeds[7], (D, D), (D // 32) ** -0.5, 1.25, ((0, 4), (1, 8)))
    bias_out = gaussian(seeds[8], (D,), 0.5, 3.0, (), jnp.float32)
    norm_gain = jnp.clip(1.0 + 0.1 * jax.random.normal(seeds[9], (D,), jnp.float32), 0.5, 1.5)
    norm_shift = gaussian(seeds[10], (D,), 0.3, 2.0, (), jnp.float32)
    weight_up = gaussian(seeds[11], (D, FF), D ** -0.5, 0.21875, ((0, 8), (1, 4)))
    bias_up = gaussian(seeds[12], (FF,), 0.5, 3.0, ((0, 4),), jnp.float32)
    weight_down = gaussian(seeds[13], (FF, D), FF ** -0.5, 0.109375, ((0, 4), (1, 8)))
    bias_down = gaussian(seeds[14], (D,), 0.3, 2.0, (), jnp.float32)
    final_gain = jnp.clip(1.0 + 0.1 * jax.random.normal(seeds[15], (D,), jnp.float32), 0.5, 1.5)
    final_shift = gaussian(seeds[16], (D,), 0.3, 2.0, (), jnp.float32)
    cotangent = gaussian_with(seeds[17], (TOKENS, D), 1.0, 6.0, ((0, 32),), (0, 1, 32, 2.75))
    return dict(inputs=inputs, doc_lengths=doc_lengths, weight_query=weight_query, weight_key=weight_key, weight_value=weight_value, bias_query=bias_query, bias_value=bias_value, weight_out=weight_out, bias_out=bias_out, norm_gain=norm_gain, norm_shift=norm_shift, weight_up=weight_up, bias_up=bias_up, weight_down=weight_down, bias_down=bias_down, final_gain=final_gain, final_shift=final_shift, cotangent=cotangent)


@jax.custom_vjp
def low(v):
    return lax.optimization_barrier(v.astype(jnp.bfloat16)).astype(jnp.float32)

@jax.custom_vjp
def low_back(v):
    return v

def low_keep(v):
    return (low(v), None)

def low_pass(kept, grad):
    return (grad,)

def back_keep(v):
    return (v, None)

def back_low(kept, grad):
    return (low(grad),)
low.defvjp(low_keep, low_pass)
low_back.defvjp(back_keep, back_low)

def matmul(left, right):
    return jnp.dot(left, right, precision=lax.Precision.HIGHEST, preferred_element_type=jnp.float32)

def segment_ids(lengths):
    ends = jnp.cumsum(lengths, axis=1)
    positions = lax.broadcasted_iota(jnp.int32, (TOK_DEV,), 0)
    return lax.optimization_barrier(jnp.sum((positions[None, :, None] >= ends[:, None, :]).astype(jnp.int32), axis=2))

def layer_norm(hidden, gain, shift):
    mean = lax.optimization_barrier(jnp.mean(hidden, axis=-1, keepdims=True))
    variance = lax.optimization_barrier(jnp.mean(hidden * hidden, axis=-1, keepdims=True)) - mean * mean
    return (hidden - mean) * lax.rsqrt(variance + 1e-12) * gain + shift

def attend(parts):
    queries, keys, values, segments = parts
    scores = jnp.einsum('qhd,khd->hqk', queries, keys, precision=lax.Precision.HIGHEST) * HEAD_DIM ** (-0.5)
    scores = low_back(scores)
    mask = segments[:, None] == segments[None, :]
    scores = jnp.where(mask[None], scores, -1000000000.0)
    summit = lax.optimization_barrier(jnp.max(scores, axis=-1, keepdims=True))
    exponent = jnp.exp(scores - summit)
    probs = exponent / lax.optimization_barrier(jnp.sum(exponent, axis=-1, keepdims=True))
    return jnp.einsum('hqk,khd->qhd', low(probs), values, precision=lax.Precision.HIGHEST)

def layer(inputs, weight_query, weight_key, weight_value, bias_query, bias_value, weight_out, bias_out, norm_gain, norm_shift, weight_up, bias_up, weight_down, bias_down, final_gain, final_shift, segments):
    queries = low(low_back(matmul(inputs, weight_query)) + bias_query)
    keys = low(low_back(matmul(inputs, weight_key)))
    values = low(low_back(matmul(inputs, weight_value)) + bias_value)
    shape = (SEQS, TOK_DEV, HEADS, HEAD_DIM)
    attended = lax.map(jax.checkpoint(attend), (queries.reshape(shape), keys.reshape(shape), values.reshape(shape), segments))
    attended = low(low_back(attended.reshape(TOKENS, D)))
    first = inputs + low_back(matmul(attended, weight_out)) + bias_out
    normed = layer_norm(first, norm_gain, norm_shift)
    upper = low_back(matmul(low(normed), weight_up)) + bias_up
    active = low(jax.nn.gelu(upper, approximate=False))
    second = normed + low_back(matmul(active, weight_down)) + bias_down
    return layer_norm(second, final_gain, final_shift)

def reference(inputs, doc_lengths, weight_query, weight_key, weight_value, bias_query, bias_value, weight_out, bias_out, norm_gain, norm_shift, weight_up, bias_up, weight_down, bias_down, final_gain, final_shift, cotangent):
    segments = segment_ids(doc_lengths)
    floats = (inputs, weight_query, weight_key, weight_value, bias_query, bias_value, weight_out, bias_out, norm_gain, norm_shift, weight_up, bias_up, weight_down, bias_down, final_gain, final_shift)
    floats = tuple((item.astype(jnp.float32) for item in floats))

    def whole(*params):
        return layer(*params, segments)
    result, pull = jax.vjp(whole, *floats)
    grads = pull(cotangent.astype(jnp.float32))
    return (result.astype(jnp.bfloat16), grads[0], grads[1], grads[2], grads[3], grads[4], grads[5], grads[6], grads[7], grads[8], grads[9], grads[10], grads[11], grads[12], grads[13], grads[14], grads[15])
```

```python
from functools import partial

import jax
import jax.numpy as jnp
from jax import lax
from jax.sharding import PartitionSpec as P

HEAD_DIM = 64


masked_score = -1000000000.0
norm_eps = 1e-12
low = jnp.bfloat16


def dot(left, right, dims):
    return lax.dot_general(left, right, ((dims[:1], dims[1:]), ((), ())), preferred_element_type=jnp.float32)


class Whole:
    partial_type = jnp.float32

    def __init__(self, mesh):
        self.rows = mesh.shape["row"]
        self.cols = mesh.shape["col"]

    def token_blocks(self):
        return [jnp.int32(block) for block in range(self.cols)]

    def gather_rows(self, part):
        return lax.all_gather(part, "row", axis=0, tiled=True)

    def scatter_rows(self, full):
        return lax.psum_scatter(full, "row", scatter_dimension=0, tiled=True)

    def gather_tokens(self, part):
        return lax.all_gather(part, "col", axis=0, tiled=True)

    def scatter_tokens(self, full):
        return lax.psum_scatter(full, "col", scatter_dimension=0, tiled=True)

    def sum_cols(self, item):
        return lax.psum(item, "col")

    def sum_rows(self, item):
        return lax.psum(item, "row")


class Box(Whole):
    partial_type = low

    def places(self):
        row, col = lax.axis_index("row"), lax.axis_index("col")
        return row // 2, row % 2, col // 2, col % 2

    def move(self, item, to):
        pairs = []
        for device in range(32):
            z, x, y, c = device // 8, device // 4 % 2, device // 2 % 2, device % 2
            z, x, y, c = to(z, x, y, c)
            pairs.append((device, z * 8 + x * 4 + y * 2 + c))
        return lax.ppermute(item, ("row", "col"), pairs)

    def swap_x(self, item):
        return self.move(item, lambda z, x, y, c: (z, 1 - x, y, c))

    def swap_y(self, item):
        return self.move(item, lambda z, x, y, c: (z, x, 1 - y, c))

    def swap_c(self, item):
        return self.move(item, lambda z, x, y, c: (z, x, y, 1 - c))

    def swap_z(self, item, bit):
        return self.move(item, lambda z, x, y, c: (z ^ bit, x, y, c))

    def ring_z(self, item):
        after = {0: 1, 1: 3, 3: 2, 2: 0}
        return self.move(item, lambda z, x, y, c: (after[z], x, y, c))

    def token_blocks(self):
        _, _, y, c = self.places()
        return [2 * y + c, 2 * (1 - y) + c, 2 * y + 1 - c, 2 * (1 - y) + 1 - c]

    def gather_rows(self, part):
        z, x, _, _ = self.places()
        place = z ^ (z >> 1)
        held = jnp.zeros((4,) + part.shape, part.dtype)
        held = lax.dynamic_update_slice(held, part[None], (z, 0, 0))
        block = part
        for step in (1, 2, 3):
            block = self.ring_z(block)
            source = (place - step) & 3
            source = source ^ (source >> 1)
            held = lax.dynamic_update_slice(held, block[None], (source, 0, 0))
        other = self.swap_x(held)
        full = jnp.where(x == 0, jnp.stack((held, other), 1), jnp.stack((other, held), 1))
        return full.reshape((8 * part.shape[0],) + part.shape[1:])

    def scatter_rows(self, full):
        z, x, _, _ = self.places()
        place = z ^ (z >> 1)
        count = full.shape[0] // 8
        parts = full.reshape((4, 2, count) + full.shape[1:])
        theirs = jnp.where(x == 0, parts[:, 1], parts[:, 0]).astype(low)
        mine = jnp.where(x == 0, parts[:, 0], parts[:, 1]).astype(jnp.float32)
        mine = mine + self.swap_x(theirs).astype(jnp.float32)

        def own(step):
            at = (place - step) & 3
            at = at ^ (at >> 1)
            return lax.dynamic_index_in_dim(mine, at, 0, keepdims=False)

        total = own(1)
        for step in (2, 3, 4):
            total = own(step) + self.ring_z(total.astype(low)).astype(jnp.float32)
        return total

    def gather_tokens(self, part):
        pair = jnp.concatenate((part, self.swap_y(part)), axis=0)
        return jnp.concatenate((pair, self.swap_c(pair)), axis=0)

    def scatter_tokens(self, full):
        count = full.shape[0] // 4
        half = full[: 2 * count] + self.swap_c(full[2 * count :].astype(low)).astype(jnp.float32)
        return half[:count] + self.swap_y(half[count:].astype(low)).astype(jnp.float32)

    def sum_cols(self, item):
        item = item + self.swap_c(item)
        return item + self.swap_y(item)

    def sum_rows(self, item):
        item = item + self.swap_x(item)
        item = item + self.swap_z(item, 1)
        return item + self.swap_z(item, 2)


def norm_forward(hidden, gain, shift):
    width = hidden.shape[1]
    mean = jnp.sum(hidden, axis=1) / width
    variance = jnp.sum(hidden * hidden, axis=1) / width - mean * mean
    scale = lax.rsqrt(variance + norm_eps)
    centred = (hidden - mean[:, None]) * scale[:, None]
    return (centred * gain + shift, centred, scale)


def norm_backward(grad, centred, scale, gain):
    width = grad.shape[1]
    scaled = grad * gain
    first_sum = jnp.sum(scaled, axis=1)
    second_sum = jnp.sum(scaled * centred, axis=1)
    return scale[:, None] * (
        scaled - first_sum[:, None] / width - centred * (second_sum[:, None] / width)
    )


def block_scores(rows, row_segments, keys, segments):
    scores = jnp.einsum(
        "qhd,khd->hqk", rows, keys, preferred_element_type=jnp.float32
    ) * HEAD_DIM ** (-0.5)
    mask = row_segments[:, None] == segments[None, :]
    return jnp.where(mask[None], scores, masked_score)


def attention_forward(queries, keys, values, segments):
    count = queries.shape[0]
    block = min(512, count)

    def one_block(index):
        start = index * block
        rows = lax.dynamic_slice_in_dim(queries, start, block, 0)
        row_segments = lax.dynamic_slice_in_dim(segments, start, block, 0)
        scores = block_scores(rows, row_segments, keys, segments)
        summit = jnp.max(scores, axis=2, keepdims=True)
        exponent = jnp.exp(scores - summit)
        total = jnp.sum(exponent, axis=2, keepdims=True)
        probs = (exponent / total).astype(jnp.bfloat16)
        mixed = jnp.einsum("hqk,khd->qhd", probs, values, preferred_element_type=jnp.float32)
        return (mixed, (summit + jnp.log(total))[:, :, 0])

    mixed, logsum = lax.map(one_block, jnp.arange(count // block))
    return (mixed.reshape(count, -1), logsum)


def attention_backward(queries, keys, values, segments, logsum, grad_mixed):
    count = queries.shape[0]
    block = min(512, count)
    scale = HEAD_DIM ** (-0.5)

    def one_block(carry, index):
        grad_keys, grad_values = carry
        start = index * block
        rows = lax.dynamic_slice_in_dim(queries, start, block, 0)
        row_segments = lax.dynamic_slice_in_dim(segments, start, block, 0)
        row_grads = lax.dynamic_slice_in_dim(grad_mixed, start, block, 0)
        scores = block_scores(rows, row_segments, keys, segments)
        probs = jnp.exp(scores - logsum[index][:, :, None])
        low_probs = probs.astype(jnp.bfloat16)
        grad_values = grad_values + jnp.einsum(
            "hqk,qhd->khd", low_probs, row_grads, preferred_element_type=jnp.float32
        )
        grad_probs = jnp.einsum(
            "qhd,khd->hqk", row_grads, values, preferred_element_type=jnp.float32
        )
        inner = jnp.sum(grad_probs * probs, axis=2, keepdims=True)
        grad_scores = (probs * (grad_probs - inner)).astype(jnp.bfloat16)
        grad_rows = (
            jnp.einsum("hqk,khd->qhd", grad_scores, keys, preferred_element_type=jnp.float32)
            * scale
        )
        grad_keys = (
            grad_keys
            + jnp.einsum("hqk,qhd->khd", grad_scores, rows, preferred_element_type=jnp.float32)
            * scale
        )
        return ((grad_keys, grad_values), grad_rows)

    zeros = jnp.zeros(keys.shape, jnp.float32)
    (grad_keys, grad_values), grad_queries = lax.scan(
        one_block, (zeros, zeros), jnp.arange(count // block)
    )
    return (
        grad_queries.reshape(count, -1),
        grad_keys.reshape(count, -1),
        grad_values.reshape(count, -1),
    )


def local(
    comm,
    inputs,
    doc_lengths,
    weight_query,
    weight_key,
    weight_value,
    bias_query,
    bias_value,
    weight_out,
    bias_out,
    norm_gain,
    norm_shift,
    weight_up,
    bias_up,
    weight_down,
    bias_down,
    final_gain,
    final_shift,
    cotangent,
):
    own = inputs.shape[0]
    count = own * comm.cols
    ends = jnp.cumsum(doc_lengths, axis=1)
    steps = jnp.arange(own, dtype=jnp.int32)
    positions = jnp.concatenate([block * own + steps for block in comm.token_blocks()])
    segments = jnp.sum((positions[:, None] >= ends).astype(jnp.int32), axis=1)

    width = weight_query.shape[1]
    heads = width // HEAD_DIM
    attn_part = jnp.concatenate((weight_query, weight_key, weight_value, weight_out.T), axis=1)
    attn_w = comm.gather_rows(attn_part)
    features = comm.gather_tokens(inputs)
    up_w = comm.gather_rows(weight_up)
    down_t = comm.gather_rows(weight_down.T)
    joined = attn_w[:, : 3 * width]
    out_t = attn_w[:, 3 * width :]

    projected = dot(features, joined, (1, 0))
    shape = (count, heads, HEAD_DIM)
    queries = (projected[:, :width] + bias_query).astype(low).reshape(shape)
    keys = projected[:, width : 2 * width].astype(low).reshape(shape)
    values = (projected[:, 2 * width :] + bias_value).astype(low).reshape(shape)
    mixed, logsum = attention_forward(queries, keys, values, segments)
    attended = mixed.astype(low)
    branch = comm.scatter_tokens(dot(attended, out_t, (1, 1)))
    first = inputs.astype(jnp.float32) + branch + bias_out
    normed, centred_one, scale_one = norm_forward(first, norm_gain, norm_shift)
    middle = comm.gather_tokens(normed.astype(low))
    upper = dot(middle, up_w, (1, 0)) + bias_up
    active = jax.nn.gelu(upper, approximate=False).astype(low)
    down_sum = comm.scatter_tokens(dot(active, down_t, (1, 1)))
    second = normed + down_sum + bias_down
    result, centred_two, scale_two = norm_forward(second, final_gain, final_shift)

    grad_result = cotangent.astype(jnp.float32)
    grad_final_gain = jnp.sum(grad_result * centred_two, axis=0)
    grad_final_shift = jnp.sum(grad_result, axis=0)
    grad_second = norm_backward(grad_result, centred_two, scale_two, final_gain)
    grad_down_bias = jnp.sum(grad_second, axis=0)
    second_full = comm.gather_tokens(grad_second.astype(low))
    grad_down_t = comm.scatter_rows(dot(second_full, active, (0, 0)).astype(comm.partial_type))
    grad_active = dot(second_full, down_t, (1, 0))
    _, gelu_pull = jax.vjp(partial(jax.nn.gelu, approximate=False), upper)
    grad_upper = gelu_pull(grad_active)[0]
    grad_up_bias = jnp.sum(grad_upper, axis=0)
    low_upper = grad_upper.astype(low)
    grad_up = comm.scatter_rows(dot(middle, low_upper, (0, 0)).astype(comm.partial_type))
    grad_normed = grad_second + comm.scatter_tokens(dot(low_upper, up_w, (1, 1)))
    grad_norm_gain = jnp.sum(grad_normed * centred_one, axis=0)
    grad_norm_shift = jnp.sum(grad_normed, axis=0)
    grad_first = norm_backward(grad_normed, centred_one, scale_one, norm_gain)
    grad_out_bias = jnp.sum(grad_first, axis=0)

    everywhere = jnp.stack(
        (
            grad_out_bias,
            grad_norm_gain,
            grad_norm_shift,
            grad_down_bias,
            grad_final_gain,
            grad_final_shift,
        )
    )
    size = everywhere.shape[1]
    flat = jnp.concatenate((comm.sum_cols(everywhere).reshape(-1), grad_up_bias))
    flat = comm.sum_rows(flat)
    everywhere = flat[: 6 * size].reshape(6, size)
    grad_up_bias = flat[6 * size :]

    first_full = comm.gather_tokens(grad_first.astype(low))
    grad_out_t = dot(first_full, attended, (0, 0))
    grad_mixed = dot(first_full, out_t, (1, 0)).astype(low).reshape(shape)
    grad_queries, grad_keys, grad_values = attention_backward(
        queries, keys, values, segments, logsum, grad_mixed
    )
    biases = comm.sum_rows(
        jnp.concatenate((jnp.sum(grad_queries, axis=0), jnp.sum(grad_values, axis=0)))
    )
    grad_joined = jnp.concatenate((grad_queries, grad_keys, grad_values), axis=1).astype(low)
    grad_attn = comm.scatter_rows(
        jnp.concatenate((dot(features, grad_joined, (0, 0)), grad_out_t), axis=1).astype(comm.partial_type)
    )
    grad_input = grad_first + comm.scatter_tokens(dot(grad_joined, joined, (1, 1)))
    return (
        result.astype(low),
        grad_input,
        grad_attn[:, :width].astype(jnp.float32),
        grad_attn[:, width : 2 * width].astype(jnp.float32),
        grad_attn[:, 2 * width : 3 * width].astype(jnp.float32),
        biases[:width],
        biases[width:],
        grad_attn[:, 3 * width :].astype(jnp.float32).T,
        everywhere[0],
        everywhere[1],
        everywhere[2],
        grad_up.astype(jnp.float32),
        grad_up_bias,
        grad_down_t.astype(jnp.float32).T,
        everywhere[3],
        everywhere[4],
        everywhere[5],
    )


def solution(mesh):
    small = (mesh.shape["row"], mesh.shape["col"]) == (8, 4)
    comm = Box(mesh) if small else Whole(mesh)
    tokens, both, turned = P(("row", "col"), None), P("row", "col"), P("col", "row")
    placed = (
        (tokens, P("row", None), both, both, both, P("col"), P("col"), turned)
        + (P(), P(), P(), both, P("col"), turned, P(), P(), P(), tokens)
    )
    outs = (
        (tokens, tokens, both, both, both, P("col"), P("col"), turned)
        + (P(), P(), P(), both, P("col"), turned, P(), P(), P())
    )
    return jax.shard_map(
        partial(local, comm), mesh=mesh, in_specs=placed, out_specs=outs, check_vma=False
    )
```

```python
from functools import partial

import jax
import jax.numpy as jnp
from jax import lax
from jax.experimental import pallas as pl
from jax.experimental.pallas import tpu as pltpu
from jax.sharding import PartitionSpec as P

HEAD_DIM = 64
LANES = 256
TILE = 256


norm_eps = 1e-12
low = jnp.bfloat16


def dot(left, right, dims):
    return lax.dot_general(
        left, right, ((dims[:1], dims[1:]), ((), ())), preferred_element_type=jnp.float32
    )


def wide(item):
    return item.astype(jnp.float32)


class Whole:
    partial_type = jnp.float32

    def __init__(self, mesh):
        self.cols = mesh.shape["col"]

    def token_blocks(self):
        return [jnp.int32(block) for block in range(self.cols)]

    def gather_rows(self, part, name):
        return lax.all_gather(part, "row", axis=0, tiled=True)

    def gather_blocks(self, up, down):
        return [self.gather_rows(up, "")], [self.gather_rows(down, "")]

    def spread(self, item):
        return [item]

    def scatter_rows(self, full, name):
        return lax.psum_scatter(full, "row", scatter_dimension=0, tiled=True)

    def scatter_blocks(self, blocks, y_first, name):
        return self.scatter_rows(blocks[0], name)

    def gather_tokens(self, part, name):
        return lax.all_gather(part, "col", axis=0, tiled=True)

    def scatter_tokens(self, full, name):
        return lax.psum_scatter(full, "col", scatter_dimension=0, tiled=True)

    def gather_near(self, part, name):
        return self.gather_tokens(part, name)

    def scatter_near(self, full, name):
        return self.scatter_tokens(full, name)

    def sum_smalls(self, everywhere, blocks):
        return lax.psum(everywhere, ("row", "col")), lax.psum(blocks[0], "row")

    def sum_rows(self, item):
        return lax.psum(item, "row")


class Box(Whole):
    partial_type = low

    def places(self):
        row, col = lax.axis_index("row"), lax.axis_index("col")
        return row // 2, row % 2, col // 2, col % 2

    def move(self, item, to, name):
        pairs = []
        for device in range(32):
            z, x, y, c = device // 8, device // 4 % 2, device // 2 % 2, device % 2
            z, x, y, c = to(z, x, y, c)
            pairs.append((device, z * 8 + x * 4 + y * 2 + c))
        with jax.named_scope(name):
            return lax.ppermute(item, ("row", "col"), pairs)

    def swap_x(self, item, name):
        return self.move(item, lambda z, x, y, c: (z, 1 - x, y, c), name)

    def swap_y(self, item, name):
        return self.move(item, lambda z, x, y, c: (z, x, 1 - y, c), name)

    def swap_c(self, item, name):
        return self.move(item, lambda z, x, y, c: (z, x, y, 1 - c), name)

    def swap_z(self, item, bit, name):
        return self.move(item, lambda z, x, y, c: (z ^ bit, x, y, c), name)

    def ring_z(self, item, name):
        after = {0: 1, 1: 3, 3: 2, 2: 0}
        return self.move(item, lambda z, x, y, c: (after[z], x, y, c), name)

    def token_blocks(self):
        _, _, y, c = self.places()
        return [2 * y + c, 2 * (1 - y) + c, 2 * y + 1 - c, 2 * (1 - y) + 1 - c]

    def gather_z(self, part, name):
        z, _, _, _ = self.places()
        place = z ^ (z >> 1)
        held = jnp.zeros((4,) + part.shape, part.dtype)
        held = lax.dynamic_update_slice(held, part[None], (z, 0, 0))
        block = part
        for step in (1, 2, 3):
            block = self.ring_z(block, f"{name}_z{step}")
            source = (place - step) & 3
            source = source ^ (source >> 1)
            held = lax.dynamic_update_slice(held, block[None], (source, 0, 0))
        return held

    def woven(self, mine, theirs):
        _, x, _, _ = self.places()
        full = jnp.where(x == 0, jnp.stack((mine, theirs), 1), jnp.stack((theirs, mine), 1))
        return lax.optimization_barrier(full.reshape((-1,) + mine.shape[2:]))

    def gather_rows(self, part, name):
        held = self.gather_z(part, name)
        return self.woven(held, self.swap_x(held, f"{name}_x"))

    def gather_blocks(self, up, down):
        width = up.shape[1]
        held = self.gather_z(jnp.concatenate((up, down), axis=1), "ffn")
        up, down = held[:, :, :width], held[:, :, width:]
        up_x = self.swap_x(up, "up_x")
        down_y = self.swap_y(down, "down_y")
        up_y = self.swap_y(up, "up_y")
        down_x = self.swap_x(down, "down_x")
        up_xy = self.swap_y(up_x, "up_xy")
        down_yx = self.swap_x(down_y, "down_yx")
        return (
            [self.woven(up, up_x), self.woven(up_y, up_xy)],
            [self.woven(down, down_x), self.woven(down_y, down_yx)],
        )

    def spread(self, item):
        return [item, self.swap_y(item, "spread")]

    def reduce_z(self, mine, name):
        z, _, _, _ = self.places()
        place = z ^ (z >> 1)

        def own(step):
            at = (place - step) & 3
            at = at ^ (at >> 1)
            return lax.dynamic_index_in_dim(mine, at, 0, keepdims=False)

        total = own(1)
        for step in (2, 3, 4):
            total = wide(own(step)) + wide(self.ring_z(total.astype(low), f"{name}_z{step}"))
        return total

    def halves(self, full):
        _, x, _, _ = self.places()
        parts = full.reshape((4, 2, -1) + full.shape[1:])
        mine = jnp.where(x == 0, parts[:, 0], parts[:, 1])
        theirs = jnp.where(x == 0, parts[:, 1], parts[:, 0])
        return mine, theirs.astype(low)

    def scatter_rows(self, full, name):
        mine, theirs = self.halves(full)
        return self.reduce_z(wide(mine) + wide(self.swap_x(theirs, f"{name}_x")), name)

    def scatter_blocks(self, blocks, y_first, name):
        if y_first:
            total = wide(blocks[0]) + wide(self.swap_y(blocks[1].astype(low), f"{name}_y"))
            return self.scatter_rows(total.astype(low), name)
        near_mine, near_theirs = self.halves(blocks[0])
        far_mine, far_theirs = self.halves(blocks[1])
        far = wide(far_mine) + wide(self.swap_x(far_theirs, f"{name}_xf"))
        near = wide(near_mine) + wide(self.swap_x(near_theirs, f"{name}_xn"))
        near = near + wide(self.swap_y(far.astype(low), f"{name}_y"))
        return self.reduce_z(near, name)

    def gather_tokens(self, part, name):
        pair = jnp.concatenate((part, self.swap_y(part, f"{name}_y")), axis=0)
        return jnp.concatenate((pair, self.swap_c(pair, f"{name}_c")), axis=0)

    def scatter_tokens(self, full, name):
        count = full.shape[0] // 4
        theirs = self.swap_c(full[2 * count :].astype(low), f"{name}_c")
        half = full[: 2 * count] + wide(theirs)
        return half[:count] + wide(self.swap_y(half[count:].astype(low), f"{name}_y"))

    def gather_near(self, part, name):
        return jnp.concatenate((part, self.swap_c(part, name)), axis=0)

    def scatter_near(self, full, name):
        count = full.shape[0] // 2
        return full[:count] + wide(self.swap_c(full[count:].astype(low), name))

    def sum_rows(self, item, name="late"):
        item = item + self.swap_x(item, f"{name}_x")
        item = item + self.swap_z(item, 1, f"{name}_z1")
        return item + self.swap_z(item, 2, f"{name}_z2")

    def sum_smalls(self, everywhere, blocks):
        size = everywhere.shape[0]
        everywhere = everywhere + self.swap_c(everywhere, "small_c")
        other = self.swap_y(jnp.concatenate((everywhere, blocks[1])), "small_y")
        flat = jnp.concatenate((everywhere, blocks[0])) + other
        flat = self.sum_rows(flat, "small")
        return flat[:size], flat[size:]


def norm_forward(hidden, gain, shift):
    width = hidden.shape[1]
    mean = jnp.sum(hidden, axis=1) / width
    variance = jnp.sum(hidden * hidden, axis=1) / width - mean * mean
    scale = lax.rsqrt(variance + norm_eps)
    centred = (hidden - mean[:, None]) * scale[:, None]
    return (centred * gain + shift, centred, scale)


def norm_backward(grad, centred, scale, gain):
    width = grad.shape[1]
    scaled = grad * gain
    first_sum = jnp.sum(scaled, axis=1)
    second_sum = jnp.sum(scaled * centred, axis=1)
    return scale[:, None] * (
        scaled - first_sum[:, None] / width - centred * (second_sum[:, None] / width)
    )


def head_of(block, head, keep_from=None):
    lanes = lax.broadcasted_iota(jnp.int32, block.shape, 1)
    keep = (lanes >= head * HEAD_DIM) & (lanes < (head + 1) * HEAD_DIM)
    if keep_from is not None:
        keep = keep | (lanes >= keep_from)
    return jnp.where(keep, block, jnp.zeros_like(block))


def turned(block):
    return block.astype(jnp.float32).T


def forward_kernel(heads, qkv_ref, mixed_ref, stat_ref, values_t):
    count = qkv_ref.shape[0]
    width = heads * HEAD_DIM
    for start in range(0, count, TILE):
        values = qkv_ref[start : start + TILE, 2 * LANES : 3 * LANES]
        values_t[:, start : start + TILE] = turned(values).astype(low)
    stat_ref[...] = jnp.zeros_like(stat_ref)

    def one(index, carry):
        start = pl.multiple_of(index * TILE, TILE)
        rows = qkv_ref[pl.ds(start, TILE), :LANES]
        keys = qkv_ref[:, LANES : 2 * LANES]
        parts = []
        for head in range(heads):
            scores = dot(keys, head_of(rows, head, width), (1, 1))
            summit = jnp.max(scores, axis=0, keepdims=True)
            exponent = jnp.exp(scores - summit)
            total = jnp.sum(exponent, axis=0, keepdims=True)
            values = values_t[head * HEAD_DIM : (head + 1) * HEAD_DIM, :]
            parts.append(dot(values, exponent.astype(low), (1, 0)) / total)
            stat_ref[head : head + 1, pl.ds(start, TILE)] = summit + jnp.log(total)
        parts.append(jnp.zeros((LANES - width, TILE), jnp.float32))
        mixed_ref[pl.ds(start, TILE), :] = jnp.concatenate(parts, axis=0).T.astype(low)
        return carry

    lax.fori_loop(0, count // TILE, one, 0)


def attention_forward(qkv, heads):
    count = qkv.shape[0]
    return pl.pallas_call(
        partial(forward_kernel, heads),
        out_shape=(
            jax.ShapeDtypeStruct((count, LANES), low),
            jax.ShapeDtypeStruct((8, count), jnp.float32),
        ),
        scratch_shapes=[pltpu.VMEM((LANES, count), low)],
        cost_estimate=pl.CostEstimate(
            flops=4 * heads * count * count * LANES,
            bytes_accessed=5 * count * LANES * 2,
            transcendentals=heads * count * count,
        ),
        name="attend",
    )(qkv)


def backward_kernel(heads, qkv_ref, mixed_ref, grad_ref, stat_ref, out_ref, sum_ref,
                    probs_t, slopes_t, keys_t, inner_t, grad_rows_t, grad_keys, grad_values):
    count = qkv_ref.shape[0]
    width = heads * HEAD_DIM
    blocks = range(0, count, TILE)
    for start in blocks:
        part = slice(start, start + TILE)
        keys_t[:, part] = turned(qkv_ref[part, LANES : 2 * LANES]).astype(low)
        product = grad_ref[part, :].astype(jnp.float32) * mixed_ref[part, :].astype(jnp.float32)
        product = product.T
        for head in range(heads):
            inner_t[head : head + 1, part] = jnp.sum(
                product[head * HEAD_DIM : (head + 1) * HEAD_DIM], axis=0, keepdims=True
            )
    grad_rows_t[width:, :] = jnp.zeros((LANES - width, count), jnp.float32)

    for head in range(heads):
        def one(index, carry):
            start = pl.multiple_of(index * TILE, TILE)
            rows = head_of(qkv_ref[pl.ds(start, TILE), :LANES], head, width)
            row_grads = head_of(grad_ref[pl.ds(start, TILE), :], head)
            logsum = stat_ref[head : head + 1, pl.ds(start, TILE)]
            inner = inner_t[head : head + 1, pl.ds(start, TILE)]
            for key_start in blocks:
                part = slice(key_start, key_start + TILE)
                scores = dot(qkv_ref[part, LANES : 2 * LANES], rows, (1, 1))
                probs = jnp.exp(scores - logsum)
                grad_probs = dot(qkv_ref[part, 2 * LANES : 3 * LANES], row_grads, (1, 1))
                probs_t[part, pl.ds(start, TILE)] = probs.astype(low)
                slopes_t[part, pl.ds(start, TILE)] = (probs * (grad_probs - inner)).astype(low)
            return carry

        lax.fori_loop(0, count // TILE, one, 0)
        rows = head_of(qkv_ref[:, :LANES], head)
        row_grads = head_of(grad_ref[...], head)
        more_values = dot(probs_t[...], row_grads, (1, 0))
        more_keys = dot(slopes_t[...], rows, (1, 0))
        if head == 0:
            grad_values[...] = more_values
            grad_keys[...] = more_keys
        else:
            grad_values[...] += more_values
            grad_keys[...] += more_keys
        mine = slice(head * HEAD_DIM, (head + 1) * HEAD_DIM)
        grad_rows_t[mine, :] = dot(keys_t[mine, :], slopes_t[...], (1, 0)) * HEAD_DIM ** (-0.5)

    sums = jnp.zeros((1, LANES), jnp.float32)
    for start in blocks:
        part = slice(start, start + TILE)
        grad_rows = grad_rows_t[:, part].T
        sums = sums + jnp.sum(grad_rows, axis=0, keepdims=True)
        out_ref[part, :LANES] = grad_rows.astype(low)
        out_ref[part, LANES : 2 * LANES] = grad_keys[part, :].astype(low)
        out_ref[part, 2 * LANES :] = grad_values[part, :].astype(low)
    sum_ref[0:1, :] = sums
    sum_ref[1:2, :] = jnp.sum(grad_values[...], axis=0, keepdims=True)


def attention_backward(qkv, mixed, grad_mixed, stats, heads):
    count = qkv.shape[0]
    return pl.pallas_call(
        partial(backward_kernel, heads),
        out_shape=(
            jax.ShapeDtypeStruct((count, 3 * LANES), low),
            jax.ShapeDtypeStruct((2, LANES), jnp.float32),
        ),
        scratch_shapes=[
            pltpu.VMEM((count, count), low),
            pltpu.VMEM((count, count), low),
            pltpu.VMEM((LANES, count), low),
            pltpu.VMEM((8, count), jnp.float32),
            pltpu.VMEM((LANES, count), jnp.float32),
            pltpu.VMEM((count, LANES), jnp.float32),
            pltpu.VMEM((count, LANES), jnp.float32),
        ],
        cost_estimate=pl.CostEstimate(
            flops=10 * heads * count * count * LANES,
            bytes_accessed=9 * count * LANES * 2,
            transcendentals=heads * count * count,
        ),
        name="attend_back",
    )(qkv, mixed, grad_mixed, stats)


def packed(projected, bias, segments, width):
    lanes = lax.broadcasted_iota(jnp.int32, projected.shape, 1)
    place = lanes % LANES
    group = lanes // LANES
    inside = place < width
    same = segments[:, None] == place - width
    code = jnp.where(
        group == 0, jnp.where(same, -(2.0**30), 0.0), jnp.where(same | (group == 2), 0.0, 1.0)
    )
    scale = jnp.where(group == 0, HEAD_DIM ** (-0.5), 1.0)
    return jnp.where(inside, (projected + bias) * scale, code).astype(low)


def grouped(three, fourth):
    cut = fourth.shape[1] // 3
    parts = []
    for index, item in enumerate(three):
        parts += [item, fourth[:, index * cut : (index + 1) * cut]]
    return jnp.concatenate(parts, axis=1)


def thirds(joined, width):
    return [joined[:, index * LANES + width : (index + 1) * LANES] for index in range(3)]


def gelu_parts(upper):
    cdf = 0.5 * (1.0 + lax.erf(upper * 0.5**0.5))
    density = jnp.exp(-0.5 * upper * upper) * (2.0 * jnp.pi) ** -0.5
    return (upper * cdf).astype(low), (cdf + upper * density).astype(low)


def local(
    comm,
    inputs,
    doc_lengths,
    weight_query,
    weight_key,
    weight_value,
    bias_query,
    bias_value,
    weight_out,
    bias_out,
    norm_gain,
    norm_shift,
    weight_up,
    bias_up,
    weight_down,
    bias_down,
    final_gain,
    final_shift,
    cotangent,
):
    own = inputs.shape[0]
    width = weight_query.shape[1]
    heads = width // HEAD_DIM
    steps = jnp.arange(own, dtype=jnp.int32)
    positions = jnp.concatenate([block * own + steps for block in comm.token_blocks()])
    segments = jnp.zeros_like(positions)
    end = jnp.int32(0)
    for document in range(doc_lengths.shape[1]):
        end = end + doc_lengths[0, document]
        segments = segments + (positions >= end).astype(jnp.int32)

    joined = comm.gather_rows(
        grouped((weight_query, weight_key, weight_value), weight_out.T), "attn"
    )
    features = comm.gather_tokens(inputs, "in")
    ups, downs = comm.gather_blocks(weight_up, weight_down.T)
    up_biases = comm.spread(bias_up)
    gap = jnp.zeros((LANES - width,), jnp.float32)
    bias = jnp.concatenate((bias_query, gap, jnp.zeros_like(bias_query), gap, bias_value, gap))
    qkv = packed(dot(features, joined, (1, 0)), bias, segments, width)
    outs = thirds(joined, width)
    out_t = jnp.concatenate(outs + outs[:1], axis=1)

    mixed, stats = attention_forward(qkv, heads)
    branch = comm.scatter_tokens(dot(mixed, out_t, (1, 1)), "branch")
    first = wide(inputs) + branch + bias_out
    normed, centred_one, scale_one = norm_forward(first, norm_gain, norm_shift)
    middle = comm.gather_near(normed.astype(low), "middle")
    actives, slopes = [], []
    for up, up_bias in zip(ups, up_biases):
        active, slope = gelu_parts(dot(middle, up, (1, 0)) + up_bias)
        actives.append(active)
        slopes.append(slope)
    actives, slopes = lax.optimization_barrier((actives, slopes))
    down_sum = comm.scatter_near(
        sum(dot(active, down, (1, 1)) for active, down in zip(actives, downs)), "lower"
    )
    second = normed + down_sum + bias_down
    result, centred_two, scale_two = norm_forward(second, final_gain, final_shift)

    grad_result = wide(cotangent)
    grad_final_gain = jnp.sum(grad_result * centred_two, axis=0)
    grad_final_shift = jnp.sum(grad_result, axis=0)
    grad_second = norm_backward(grad_result, centred_two, scale_two, final_gain)
    grad_down_bias = jnp.sum(grad_second, axis=0)
    second_full = comm.gather_near(grad_second.astype(low), "second")
    grad_down_t = comm.scatter_blocks(
        [dot(second_full, active, (0, 0)).astype(comm.partial_type) for active in actives],
        True,
        "gdown",
    )
    low_uppers, grad_up_biases = [], []
    for slope, down in zip(slopes, downs):
        grad_upper = dot(second_full, down, (1, 0)) * wide(slope)
        grad_up_biases.append(jnp.sum(grad_upper, axis=0))
        low_uppers.append(grad_upper.astype(low))
    grad_up = comm.scatter_blocks(
        [dot(middle, item, (0, 0)).astype(comm.partial_type) for item in low_uppers],
        False,
        "gup",
    )
    grad_normed = grad_second + comm.scatter_near(
        sum(dot(item, up, (1, 1)) for item, up in zip(low_uppers, ups)), "gnormed"
    )
    grad_norm_gain = jnp.sum(grad_normed * centred_one, axis=0)
    grad_norm_shift = jnp.sum(grad_normed, axis=0)
    grad_first = norm_backward(grad_normed, centred_one, scale_one, norm_gain)
    grad_out_bias = jnp.sum(grad_first, axis=0)
    smalls, grad_up_bias = comm.sum_smalls(
        jnp.concatenate(
            (
                grad_out_bias,
                grad_norm_gain,
                grad_norm_shift,
                grad_down_bias,
                grad_final_gain,
                grad_final_shift,
            )
        ),
        grad_up_biases,
    )
    smalls = smalls.reshape(6, -1)

    first_full = comm.gather_tokens(grad_first.astype(low), "first")
    grad_out_t = dot(first_full, mixed, (0, 0))[:, :width]
    grad_mixed = dot(first_full, out_t, (1, 0)).astype(low)
    grad_qkv, sums = attention_backward(qkv, mixed, grad_mixed, stats, heads)
    biases = comm.sum_rows(sums[:, :width].reshape(-1))
    grad_joined = dot(features, grad_qkv, (0, 0))
    grad_joined = grouped(
        [grad_joined[:, index * LANES : index * LANES + width] for index in range(3)], grad_out_t
    )
    grad_joined = wide(comm.scatter_rows(grad_joined.astype(comm.partial_type), "gattn"))
    grad_input = grad_first + comm.scatter_tokens(dot(grad_qkv, joined, (1, 1)), "ginput")
    return (
        result.astype(low),
        grad_input,
        grad_joined[:, :width],
        grad_joined[:, LANES : LANES + width],
        grad_joined[:, 2 * LANES : 2 * LANES + width],
        biases[:width],
        biases[width:],
        jnp.concatenate(thirds(grad_joined, width), axis=1).T,
        smalls[0],
        smalls[1],
        smalls[2],
        wide(grad_up),
        grad_up_bias,
        wide(grad_down_t).T,
        smalls[3],
        smalls[4],
        smalls[5],
    )


def solution(mesh):
    boxed = (mesh.shape["row"], mesh.shape["col"]) == (8, 4)
    comm = Box(mesh) if boxed else Whole(mesh)
    tokens, both, turn = P(("row", "col"), None), P("row", "col"), P("col", "row")
    placed = (tokens, P("row", None), both, both, both, P("col"), P("col"), turn)
    placed += (P(), P(), P(), both, P("col"), turn, P(), P(), P(), tokens)
    outs = (tokens, tokens, both, both, both, P("col"), P("col"), turn)
    outs += (P(), P(), P(), both, P("col"), turn, P(), P(), P())
    return jax.shard_map(
        partial(local, comm), mesh=mesh, in_specs=placed, out_specs=outs, check_vma=False
    )
```
